32 devices in a mesh: row: 8 (over z, core), rep: 4 (over y, x).
Axes of the slice: x: 2, y: 2, z: 4, core: 2. Of those that a mesh axis runs over, the one named last changes fastest.
Arguments:
- features: bfloat16 [4096, 256], P(('row', 'rep')), may hold values from -6 to 6
- weight: bfloat16 [256, 256], replicated, may hold values from -0.375 to 0.375
- cotangent: bfloat16 [4096, 256], P(('row', 'rep')), may hold values from -6 to 6
- adjacency: bfloat16 [8, 4, 24, 128, 128], P('row', 'rep'), may hold values from -0.15625 to 0.15625
- tile_out: int32 [8, 4, 24], P('row', 'rep'), may hold values from 0 to 3
- tile_in: int32 [8, 4, 24], P('row', 'rep'), may hold values from 0 to 7
- live_count: int32 [8, 4], P('row', 'rep'), may hold values from 6 to 24, as said below
Outputs:
- activated: bfloat16 [4096, 256], P(('row', 'rep'))
- weight_grad: float32 [256, 256], replicated
- feature_grad: float32 [4096, 256], P(('row', 'rep'))
The draws below stay inside these ranges and needn't reach their ends.
Inputs may be any that keep to these rules, and one draw needn't show every extreme that they name: `live_count`: live tile slots of one device; some device has all 24 slots live in every draw.
All inputs are finite; a program needn't handle non-finite values.
Results may differ from the reference program's by a relative error of at most 0.02.
Values may be sent and summed in bfloat16 or wider, within the bound.
A program may use at most 64 MiB of HBM per device.

```python
import jax
import jax.numpy as jnp
from jax import lax

FEAT = 256
BLOCK = 128
SLOTS = 24
NODES = 4096
N_ROW = 8
N_REP = 4


def draw_live_count(key, part):
    first_key = jax.random.fold_in(key, 11)
    second_key = jax.random.fold_in(key, 23)
    counts = jax.random.randint(first_key, (N_ROW * N_REP,), SLOTS // 4, SLOTS + 1)
    chosen = jax.random.randint(second_key, (), 0, N_ROW * N_REP)
    counts = jnp.where(jnp.arange(N_ROW * N_REP) == chosen, SLOTS, counts)
    return counts.reshape(N_ROW, N_REP).astype(jnp.int32)


def with_ends(array, own_key, smallest, high):
    longest = array.shape.index(max(array.shape))
    spots = []
    for shift in (0, 1):
        where = [jax.random.randint(jax.random.fold_in(own_key, axis), (), 0, length) for axis, length in enumerate(array.shape)]
        where[longest] = (where[longest] + shift) % array.shape[longest]
        spots.append(tuple(where))
    return array.at[spots[0]].set(smallest).at[spots[1]].set(high)


def steps_of(own_key, shape, split, least, high):
    loudness = 1.0
    for dim, blocks in split:
        draws = jax.random.uniform(jax.random.fold_in(jax.random.fold_in(own_key, 6), dim), (blocks,), jnp.float32, least / len(split), high / len(split))
        loudness = loudness * jnp.repeat(jnp.exp(draws), shape[dim] // blocks).reshape((-1,) + (1,) * (len(shape) - 1 - dim))
    return loudness


def centred(rng, shape, scale, bound, pieces=(), dtype=jnp.bfloat16):
    entries = scale * jax.random.normal(rng, shape, jnp.float32)
    if pieces:
        entries = entries * steps_of(rng, shape, pieces, -0.22, 0.18)
    return jnp.clip(entries, -bound, bound).astype(dtype)


def setup_inputs(seed: int = 0) -> dict:
    key_of = jax.random.split(jax.random.key(seed), 8)
    features = centred(key_of[0], (NODES, FEAT), 1.0, 6.0, ((0, 32),))
    weight = centred(key_of[1], (FEAT, FEAT), FEAT ** -0.5, 0.375)
    cotangent = centred(key_of[2], (NODES, FEAT), 1.0, 6.0, ((0, 32),))
    adjacency = centred(key_of[3], (N_ROW, N_REP, SLOTS, BLOCK, BLOCK), (SLOTS * BLOCK // 2) ** -0.5, 0.15625, ((0, 8), (1, 4)))
    tile_out = with_ends(jax.random.randint(key_of[4], (N_ROW, N_REP, SLOTS), 0, N_REP), jax.random.fold_in(key_of[4], 1), 0, N_REP - 1).astype(jnp.int32)
    tile_in = with_ends(jax.random.randint(key_of[5], (N_ROW, N_REP, SLOTS), 0, N_ROW), jax.random.fold_in(key_of[5], 1), 0, N_ROW - 1).astype(jnp.int32)
    live_count = draw_live_count(jax.random.fold_in(key_of[7], 71), 0)
    return dict(features=features, weight=weight, cotangent=cotangent, adjacency=adjacency, tile_out=tile_out, tile_in=tile_in, live_count=live_count)


def reference(features, weight, cotangent, adjacency, tile_out, tile_in, live_count):
    blocks = features.reshape(N_ROW, N_REP, BLOCK, FEAT)
    slot_ids = jnp.arange(SLOTS)

    def device_forward(row_id, rep_id):
        tile_set = adjacency[row_id, rep_id].astype(jnp.float32)
        in_ids = tile_in[row_id, rep_id]
        out_ids = tile_out[row_id, rep_id]
        live_mask = (slot_ids < live_count[row_id, rep_id]).astype(jnp.float32)
        column = lax.dynamic_index_in_dim(blocks, rep_id, 1, keepdims=False)
        inputs = column[in_ids].astype(jnp.float32)
        products = jnp.einsum("tij,tjf->tif", tile_set, inputs)
        onehot = (out_ids[None, :] == jnp.arange(N_REP)[:, None]).astype(jnp.float32) * live_mask[None, :]
        summed = jnp.einsum("bt,tif->bif", onehot, products, precision=lax.Precision.HIGHEST)
        return summed.astype(jnp.bfloat16)

    def row_forward(row_id):
        parts = lax.map(lambda rep_id: device_forward(row_id, rep_id), jnp.arange(N_REP))
        return jnp.sum(parts.astype(jnp.float32), axis=0)

    summed_all = lax.map(row_forward, jnp.arange(N_ROW))
    aggregated = summed_all.reshape(NODES, FEAT).astype(jnp.bfloat16)
    pre = jnp.dot(aggregated, weight, preferred_element_type=jnp.float32)
    sig = jax.nn.sigmoid(pre)
    activated = (pre * sig).astype(jnp.bfloat16)
    grad_pre = (cotangent.astype(jnp.float32) * sig * (1.0 + pre * (1.0 - sig))).astype(jnp.bfloat16)
    weight_grad = jnp.dot(aggregated.T, grad_pre, preferred_element_type=jnp.float32)
    grad_rows = jnp.dot(grad_pre, weight.T, preferred_element_type=jnp.float32).astype(jnp.bfloat16)
    grad_blocks = grad_rows.reshape(N_ROW, N_REP, BLOCK, FEAT)

    def device_back(row_id, rep_id):
        tile_set = adjacency[row_id, rep_id].astype(jnp.float32)
        in_ids = tile_in[row_id, rep_id]
        out_ids = tile_out[row_id, rep_id]
        live_mask = (slot_ids < live_count[row_id, rep_id]).astype(jnp.float32)
        group_rows = lax.dynamic_index_in_dim(grad_blocks, row_id, 0, keepdims=False)
        rows_in = group_rows[out_ids].astype(jnp.float32)
        products = jnp.einsum("tji,tjf->tif", tile_set, rows_in)
        onehot = (in_ids[None, :] == jnp.arange(N_ROW)[:, None]).astype(jnp.float32) * live_mask[None, :]
        summed = jnp.einsum("qt,tif->qif", onehot, products, precision=lax.Precision.HIGHEST)
        return summed.astype(jnp.bfloat16)

    def column_back(rep_id):
        def add_row(running, row_id):
            return running + device_back(row_id, rep_id).astype(jnp.float32), None
        start = jnp.zeros((N_ROW, BLOCK, FEAT), jnp.float32)
        running, unused = lax.scan(add_row, start, jnp.arange(N_ROW))
        return running

    returned = lax.map(column_back, jnp.arange(N_REP))
    feature_grad = jnp.transpose(returned, (1, 0, 2, 3)).reshape(NODES, FEAT)
    return activated, weight_grad, feature_grad
```

```python
import functools

import jax
import jax.numpy as jnp
from jax import lax
from jax.experimental import pallas as pl
from jax.experimental.pallas import tpu as pltpu
from jax.sharding import PartitionSpec as P

MESH = pl.DeviceIdType.MESH
F32 = jnp.float32
BF16 = jnp.bfloat16


def each(first, last, step):
    if last - first <= 4:
        for index in range(first, last):
            step(index)
    else:
        lax.fori_loop(first, last, lambda index, unused: (step(index), unused)[1], 0)


def dot(left, right):
    return jnp.dot(left, right, preferred_element_type=F32)


def kernel(
    Z, C, S,
    feat_ref, weight_hbm, cot_hbm, adj_ref, tout_ref, tin_ref, live_ref,
    act_ref, wgrad_ref, fgrad_ref,
    tiles, cum, fwd_adj, bwd_adj, feat, weight_ref, cot_ref,
    acc, own_part, part_send, part_recv, grads,
    pair_send, pair_recv, ret_send, ret_recv,
    w_part, w_pair_send, w_pair_recv, w_half, w_rep_send, w_rep_recv, w_z, w_all,
    pos,
    local_sem, feat_send_sem, feat_fwd_sem, feat_recv_sem,
    part_send_sem, part_recv_sem, grad_send_sem, grad_recv_sem,
    pair_send_sem, pair_recv_sem, ret_send_sem, ret_recv_sem,
    w_pair_sem, w_rep_send_sem, w_rep_recv_sem, w_z_send_sem, w_z_recv_sem,
    w_gather_send_sem, w_gather_recv_sem, w_last_sem,
):
    r = lax.axis_index("row")
    c = lax.axis_index("rep")
    z = r // 2
    k = r % 2
    pr = 2 * z + 1 - k
    B = tiles.shape[1]
    F = feat.shape[2]

    def z_at(d):
        return (z + d) % Z

    def z_from(d):
        return (z + Z - d) % Z

    def c_at(e):
        return (c + e) % C

    def c_from(e):
        return (c + C - e) % C

    def remote(src, dst, send_sem, recv_sem, **where):
        return pltpu.make_async_remote_copy(
            src_ref=src, dst_ref=dst, send_sem=send_sem, recv_sem=recv_sem,
            device_id=where, device_id_type=MESH,
        )

    def to_partner(src, dst, send_sem, recv_sem):
        return remote(src, dst, send_sem, recv_sem, row=pr)

    own_copy = pltpu.make_async_copy(feat_ref, feat.at[r], local_sem.at[0])
    tile_copy = pltpu.make_async_copy(adj_ref.at[0, 0], tiles, local_sem.at[1])
    weight_copy = pltpu.make_async_copy(weight_hbm, weight_ref, local_sem.at[2])
    cot_copy = pltpu.make_async_copy(cot_hbm, cot_ref, local_sem.at[3])
    own_copy.start()
    tile_copy.start()
    weight_copy.start()
    cot_copy.start()

    barrier = pltpu.get_barrier_semaphore()

    def greet(**where):
        pl.semaphore_signal(barrier, inc=1, device_id=where, device_id_type=MESH)

    greet(row=pr)
    each(1, Z, lambda d: greet(row=2 * z_at(d) + k))
    each(1, C, lambda e: greet(rep=c_at(e)))
    pl.semaphore_wait(barrier, 1 + (Z - 1) + (C - 1))

    def feat_send(d):
        return remote(
            feat_ref, feat.at[r], feat_send_sem.at[d], feat_recv_sem.at[r],
            row=2 * z_at(d) + k,
        )

    def feat_forward(d):
        q = 2 * z_from(d) + k
        return to_partner(feat.at[q], feat.at[q], feat_fwd_sem.at[d], feat_recv_sem.at[q])

    def feat_wait(q):
        to_partner(feat.at[q], feat.at[q], feat_fwd_sem.at[0], feat_recv_sem.at[q]).wait_recv()

    feat_pair = to_partner(feat_ref, feat.at[r], feat_fwd_sem.at[0], feat_recv_sem.at[r])
    each(1, Z, lambda d: feat_send(d).start())
    feat_pair.start()

    live = live_ref[0, 0]
    for s in range(S):
        pos[s] = jnp.where(s < live, tin_ref[0, 0, s] * C + tout_ref[0, 0, s], -1)
    tile_copy.wait()
    cum[S] = jnp.zeros((B, B), F32)
    for s in range(S):
        prev = jnp.int32(S)
        for other in range(s):
            prev = jnp.where(pos[other] == pos[s], other, prev)
        term = tiles[s].astype(F32)
        cum[s] = term + cum[prev] if s else term

    def place(zz, unused):
        for kk in range(2):
            for b in range(C):
                spot = (2 * zz + kk) * C + b
                last = jnp.int32(S)
                for s in range(S):
                    last = jnp.where(pos[s] == spot, s, last)
                block = cum[last]
                fwd_adj[zz, b * B:(b + 1) * B, kk * B:(kk + 1) * B] = block.astype(BF16)
                bwd_adj[2 * zz + kk, :, b * B:(b + 1) * B] = block.T.astype(BF16)
        return unused

    lax.fori_loop(0, Z, place, 0)

    def pair_feats(zz):
        return feat[pl.ds(2 * zz, 2)].reshape(2 * B, F)

    own_copy.wait()
    feat_wait(pr)
    acc[...] = dot(fwd_adj[z], pair_feats(z))

    def take(d):
        feat_wait(2 * z_from(d) + k)
        feat_forward(d).start()

    take(1)

    def add_chip(d):
        take(d + 1)
        zz = z_from(d)
        feat_wait(2 * zz + 1 - k)
        acc[...] += dot(fwd_adj[zz], pair_feats(zz))

    each(1, Z - 1, add_chip)
    end = z_from(Z - 1)
    feat_wait(2 * end + 1 - k)

    def part_of(b):
        rows = pl.ds(pl.multiple_of(b * B, B), B)
        return acc[rows] + dot(fwd_adj[end, rows], pair_feats(end))

    def part_copy(e):
        return remote(
            part_send.at[e], part_recv.at[c], part_send_sem.at[e], part_recv_sem.at[c],
            rep=c_at(e),
        )

    def send_part(e):
        part_send[e] = part_of(c_at(e)).astype(BF16)
        part_copy(e).start()

    each(1, C, send_part)
    own_part[...] = part_of(c)

    def add_part(e):
        src = c_from(e)
        remote(
            part_send.at[e], part_recv.at[src], part_send_sem.at[e], part_recv_sem.at[src],
            rep=c_at(e),
        ).wait_recv()
        own_part[...] += part_recv[src].astype(F32)

    weight_copy.wait()
    cot_copy.wait()
    each(1, C, add_part)

    agg = own_part[...].astype(BF16)
    weight = weight_ref[...]
    pre = dot(agg, weight)
    sig = jax.nn.sigmoid(pre)
    grad_pre = (cot_ref[...].astype(F32) * sig * (1.0 + pre * (1.0 - sig))).astype(BF16)
    grads[c] = lax.dot_general(
        grad_pre, weight, (((1,), (1,)), ((), ())), preferred_element_type=F32
    ).astype(BF16)

    def grad_copy(e):
        return remote(
            grads.at[c], grads.at[c], grad_send_sem.at[e], grad_recv_sem.at[c], rep=c_at(e)
        )

    each(1, C, lambda e: grad_copy(e).start())
    act_ref[...] = (pre * sig).astype(BF16)

    w_part[...] = lax.dot_general(
        agg, grad_pre, (((0,), (0,)), ((), ())), preferred_element_type=F32
    ).reshape(w_part.shape)
    w_pair_send[...] = w_part[1 - k].astype(BF16)
    w_pair = to_partner(w_pair_send, w_pair_recv, w_pair_sem.at[0], w_pair_sem.at[1])
    w_pair.start()
    w_pair.wait_recv()
    w_half[...] = w_part[k] + w_pair_recv[...].astype(F32)
    w_rep_send[...] = w_half[...].astype(BF16)

    def w_rep_copy(e):
        dst = c_at(e)
        return remote(
            w_rep_send.at[dst], w_rep_recv.at[c], w_rep_send_sem.at[e], w_rep_recv_sem.at[c],
            rep=dst,
        )

    each(1, C, lambda e: w_rep_copy(e).start())

    def grad_wait(e):
        src = c_from(e)
        remote(
            grads.at[src], grads.at[src], grad_send_sem.at[e], grad_recv_sem.at[src], rep=c_at(e)
        ).wait_recv()

    each(1, C, grad_wait)

    def returned(q):
        return dot(bwd_adj[q], grads[...].reshape(C * B, F))

    def pair_copy(j):
        zz = z_at(j)
        return to_partner(
            pair_send.at[zz], pair_recv.at[zz], pair_send_sem.at[zz], pair_recv_sem.at[zz]
        )

    def send_pair(j):
        zz = z_at(j)
        pair_send[zz] = returned(2 * zz + 1 - k).astype(BF16)
        pair_copy(j).start()

    each(1, Z + 1, send_pair)

    def add_w_rep(e):
        src = c_from(e)
        remote(
            w_rep_send.at[src], w_rep_recv.at[src], w_rep_send_sem.at[e], w_rep_recv_sem.at[src],
            rep=src,
        ).wait_recv()
        w_half[c] += w_rep_recv[src].astype(F32)

    each(1, C, add_w_rep)
    w_z[z] = w_half[c].astype(BF16)

    def w_z_copy(d):
        return remote(
            w_z.at[z], w_z.at[z], w_z_send_sem.at[d], w_z_recv_sem.at[z], row=2 * z_at(d) + k
        )

    each(1, Z, lambda d: w_z_copy(d).start())

    def joined(j):
        zz = z_at(j)
        value = returned(2 * zz + k)
        pair_copy(j).wait_recv()
        return value + pair_recv[zz].astype(F32)

    def ret_copy(d):
        return remote(
            ret_send.at[d], ret_recv.at[z], ret_send_sem.at[d], ret_recv_sem.at[z],
            row=2 * z_at(d) + k,
        )

    def send_ret(d):
        ret_send[d] = joined(d).astype(BF16)
        ret_copy(d).start()

    each(1, Z, send_ret)
    fgrad_ref[...] = joined(Z)

    def w_z_wait(d):
        src = z_from(d)
        remote(
            w_z.at[src], w_z.at[src], w_z_send_sem.at[d], w_z_recv_sem.at[src],
            row=2 * src + k,
        ).wait_recv()

    each(1, Z, w_z_wait)
    w_all[k, c] = jnp.sum(w_z[...].astype(F32), axis=0).astype(BF16)

    def w_gather_copy(e):
        return remote(
            w_all.at[k, c], w_all.at[k, c], w_gather_send_sem.at[e], w_gather_recv_sem.at[c],
            rep=c_at(e),
        )

    each(1, C, lambda e: w_gather_copy(e).start())

    def w_gather_wait(e):
        src = c_from(e)
        remote(
            w_all.at[k, src], w_all.at[k, src], w_gather_send_sem.at[e],
            w_gather_recv_sem.at[src], rep=src,
        ).wait_recv()

    each(1, C, w_gather_wait)
    w_last = to_partner(w_all.at[k], w_all.at[k], w_last_sem.at[0], w_last_sem.at[1])
    w_last.start()
    to_partner(w_all.at[1 - k], w_all.at[1 - k], w_last_sem.at[0], w_last_sem.at[1]).wait_recv()
    wgrad_ref[...] = w_all[...].astype(F32).reshape(wgrad_ref.shape)

    def add_ret(d):
        src = z_from(d)
        remote(
            ret_send.at[d], ret_recv.at[src], ret_send_sem.at[d], ret_recv_sem.at[src],
            row=2 * src + k,
        ).wait_recv()
        fgrad_ref[...] += ret_recv[src].astype(F32)

    each(1, Z, add_ret)

    feat_pair.wait_send()
    w_pair.wait_send()
    w_last.wait_send()
    pair_copy(Z).wait_send()

    def drain_z(d):
        feat_send(d).wait_send()
        feat_forward(d).wait_send()
        pair_copy(d).wait_send()
        w_z_copy(d).wait_send()
        ret_copy(d).wait_send()

    def drain_c(e):
        part_copy(e).wait_send()
        grad_copy(e).wait_send()
        w_rep_copy(e).wait_send()
        w_gather_copy(e).wait_send()

    each(1, Z, drain_z)
    each(1, C, drain_c)


def solution(mesh):
    R = mesh.shape["row"]
    C = mesh.shape["rep"]
    Z = R // 2

    def body(features, weight, cotangent, adjacency, tile_out, tile_in, live_count):
        B, F = features.shape
        S = adjacency.shape[2]
        H = F // (2 * C)
        anywhere = pl.BlockSpec(memory_space=pl.ANY)
        scalar = pl.BlockSpec(memory_space=pltpu.SMEM)
        vector = pl.BlockSpec(memory_space=pltpu.VMEM)
        dma = pltpu.SemaphoreType.DMA
        return pl.pallas_call(
            functools.partial(kernel, Z, C, S),
            out_shape=(
                jax.ShapeDtypeStruct((B, F), BF16),
                jax.ShapeDtypeStruct(weight.shape, F32),
                jax.ShapeDtypeStruct((B, F), F32),
            ),
            in_specs=[anywhere] * 4 + [scalar] * 3,
            out_specs=(vector, vector, vector),
            scratch_shapes=[
                pltpu.VMEM((S, B, B), BF16),
                pltpu.VMEM((S + 1, B, B), F32),
                pltpu.VMEM((Z, C * B, 2 * B), BF16),
                pltpu.VMEM((R, B, C * B), BF16),
                pltpu.VMEM((R, B, F), BF16),
                pltpu.VMEM(weight.shape, BF16),
                pltpu.VMEM((B, F), BF16),
                pltpu.VMEM((C * B, F), F32),
                pltpu.VMEM((B, F), F32),
                pltpu.VMEM((C, B, F), BF16),
                pltpu.VMEM((C, B, F), BF16),
                pltpu.VMEM((C, B, F), BF16),
                pltpu.VMEM((Z, B, F), BF16),
                pltpu.VMEM((Z, B, F), BF16),
                pltpu.VMEM((Z, B, F), BF16),
                pltpu.VMEM((Z, B, F), BF16),
                pltpu.VMEM((2, C, H, F), F32),
                pltpu.VMEM((C, H, F), BF16),
                pltpu.VMEM((C, H, F), BF16),
                pltpu.VMEM((C, H, F), F32),
                pltpu.VMEM((C, H, F), BF16),
                pltpu.VMEM((C, H, F), BF16),
                pltpu.VMEM((Z, H, F), BF16),
                pltpu.VMEM((2, C, H, F), BF16),
                pltpu.SMEM((S,), jnp.int32),
                dma((4,)), dma((Z,)), dma((Z,)), dma((R,)),
                dma((C,)), dma((C,)), dma((C,)), dma((C,)),
                dma((Z,)), dma((Z,)), dma((Z,)), dma((Z,)),
                dma((2,)), dma((C,)), dma((C,)), dma((Z,)), dma((Z,)),
                dma((C,)), dma((C,)), dma((2,)),
            ],
            compiler_params=pltpu.CompilerParams(
                collective_id=0, has_side_effects=True, vmem_limit_bytes=60 * 2 ** 20
            ),
        )(features, weight, cotangent, adjacency, tile_out, tile_in, live_count)

    return jax.shard_map(
        body,
        mesh=mesh,
        in_specs=(
            P(("row", "rep"), None),
            P(),
            P(("row", "rep"), None),
            P("row", "rep", None, None, None),
            P("row", "rep", None),
            P("row", "rep", None),
            P("row", "rep"),
        ),
        out_specs=(P(("row", "rep"), None), P(), P(("row", "rep"), None)),
        check_vma=False,
    )
```

```python
import functools
import math

import jax
import jax.numpy as jnp
from jax import lax
from jax.experimental import pallas as pl
from jax.experimental.pallas import tpu as pltpu
from jax.sharding import PartitionSpec as P

MESH = pl.DeviceIdType.MESH
F32 = jnp.float32
BF16 = jnp.bfloat16


def each(first, last, step):
    if last - first <= 4:
        for index in range(first, last):
            step(index)
    else:
        lax.fori_loop(first, last, lambda index, unused: (step(index), unused)[1], 0)


def dot(left, right):
    return jnp.dot(left, right, preferred_element_type=F32)


def kernel(
    Z, C, S,
    feat_hbm, weight_hbm, cot_hbm, adj_hbm, tout_hbm, tin_hbm, live_ref,
    act_ref, wgrad_ref, fgrad_ref,
    tiles, cum, fwd_adj, bwd_adj, feat, weight_ref, cot_ref,
    acc, own_part, part_send, part_recv, grads,
    pair_send, pair_recv, ret_send, ret_recv,
    w_part, w_pair_send, w_pair_recv, w_half, w_rep_send, w_rep_recv, w_z, w_all,
    tout_ref, tin_ref, pos,
    local_sem, feat_send_sem, feat_fwd_sem, feat_recv_sem,
    part_send_sem, part_recv_sem, grad_send_sem, grad_recv_sem,
    pair_send_sem, pair_recv_sem, ret_send_sem, ret_recv_sem,
    w_pair_sem, w_rep_send_sem, w_rep_recv_sem, w_z_send_sem, w_z_recv_sem,
    w_gather_send_sem, w_gather_recv_sem, w_last_sem,
):
    r = lax.axis_index("row")
    c = lax.axis_index("rep")
    z = r // 2
    k = r % 2
    pr = 2 * z + 1 - k
    B = tiles.shape[1]
    W = feat.shape[3]
    halves = feat.shape[0]

    def cols(h):
        return slice(h * W, (h + 1) * W)

    def z_at(d):
        return (z + d) % Z

    def z_from(d):
        return (z + Z - d) % Z

    def c_at(e):
        return (c + e) % C

    def c_from(e):
        return (c + C - e) % C

    def remote(src, dst, send_sem, recv_sem, **where):
        return pltpu.make_async_remote_copy(
            src_ref=src, dst_ref=dst, send_sem=send_sem, recv_sem=recv_sem,
            device_id=where, device_id_type=MESH,
        )

    def to_partner(src, dst, send_sem, recv_sem):
        return remote(src, dst, send_sem, recv_sem, row=pr)

    barrier = pltpu.get_barrier_semaphore()

    def greet(**where):
        pl.semaphore_signal(barrier, inc=1, device_id=where, device_id_type=MESH)

    each(1, Z, lambda d: greet(row=2 * z_at(d) + k))
    each(1, C, lambda e: greet(rep=c_at(e)))
    greet(row=pr)

    own_copies = [
        pltpu.make_async_copy(feat_hbm.at[:, cols(h)], feat.at[h, r], local_sem.at[6 + h])
        for h in range(halves)
    ]
    tile_copy = pltpu.make_async_copy(adj_hbm.at[0, 0], tiles, local_sem.at[0])
    weight_copy = pltpu.make_async_copy(weight_hbm, weight_ref, local_sem.at[1])
    cot_copy = pltpu.make_async_copy(cot_hbm, cot_ref, local_sem.at[2])
    id_copies = [
        pltpu.make_async_copy(tout_hbm, tout_ref, local_sem.at[3]),
        pltpu.make_async_copy(tin_hbm, tin_ref, local_sem.at[4]),
    ]
    for copy in id_copies + [tile_copy] + own_copies + [weight_copy, cot_copy]:
        copy.start()
    pl.semaphore_wait(barrier, 1 + (Z - 1) + (C - 1))

    def feat_send(h, d):
        return remote(
            feat_hbm.at[:, cols(h)], feat.at[h, r], feat_send_sem.at[h, d],
            feat_recv_sem.at[h, r], row=2 * z_at(d) + k,
        )

    def feat_forward(h, d):
        q = 2 * z_from(d) + k
        return to_partner(
            feat.at[h, q], feat.at[h, q], feat_fwd_sem.at[h, d], feat_recv_sem.at[h, q]
        )

    def feat_wait(h, q):
        to_partner(
            feat.at[h, q], feat.at[h, q], feat_fwd_sem.at[h, 0], feat_recv_sem.at[h, q]
        ).wait_recv()

    feat_pairs = [
        to_partner(
            feat_hbm.at[:, cols(h)], feat.at[h, r], feat_fwd_sem.at[h, 0], feat_recv_sem.at[h, r]
        )
        for h in range(halves)
    ]
    for h in range(halves):
        each(1, Z, lambda d: feat_send(h, d).start())
        feat_pairs[h].start()

    for copy in id_copies:
        copy.wait()
    live = live_ref[0, 0]
    for s in range(S):
        pos[s] = jnp.where(s < live, tin_ref[0, 0, s] * C + tout_ref[0, 0, s], -1)
    tile_copy.wait()
    cum[S] = jnp.zeros((B, B), F32)
    for s in range(S):
        prev = jnp.int32(S)
        for other in range(s):
            prev = jnp.where(pos[other] == pos[s], other, prev)
        term = tiles[s].astype(F32)
        cum[s] = term + cum[prev] if s else term

    def place(zz, unused):
        for kk in range(2):
            for b in range(C):
                spot = (2 * zz + kk) * C + b
                last = jnp.int32(S)
                for s in range(S):
                    last = jnp.where(pos[s] == spot, s, last)
                block = cum[last]
                fwd_adj[zz, b * B:(b + 1) * B, kk * B:(kk + 1) * B] = block.astype(BF16)
                bwd_adj[2 * zz + kk, :, b * B:(b + 1) * B] = block.T.astype(BF16)
        return unused

    lax.fori_loop(0, Z, place, 0)

    def pair_feats(h, zz):
        return feat[h, pl.ds(2 * zz, 2)].reshape(2 * B, W)

    def part_copy(h, e):
        return remote(
            part_send.at[h, e], part_recv.at[h, c], part_send_sem.at[h, e],
            part_recv_sem.at[h, c], rep=c_at(e),
        )

    end = z_from(Z - 1)
    for h in range(halves):
        own_copies[h].wait()
        feat_wait(h, pr)
        acc[...] = dot(fwd_adj[z], pair_feats(h, z))

        def take(d):
            feat_wait(h, 2 * z_from(d) + k)
            feat_forward(h, d).start()

        def add_chip(d):
            take(d + 1)
            zz = z_from(d)
            feat_wait(h, 2 * zz + 1 - k)
            acc[...] += dot(fwd_adj[zz], pair_feats(h, zz))

        take(1)
        each(1, Z - 1, add_chip)
        feat_wait(h, 2 * end + 1 - k)

        def part_of(b):
            rows = pl.ds(pl.multiple_of(b * B, B), B)
            return acc[rows] + dot(fwd_adj[end, rows], pair_feats(h, end))

        def send_part(e):
            part_send[h, e] = part_of(c_at(e)).astype(BF16)
            part_copy(h, e).start()

        each(1, C, send_part)
        own_part[h] = part_of(c)

    weight_copy.wait()
    cot_copy.wait()
    weight = weight_ref[...]
    pre = None
    agg_halves = []
    for h in range(halves):

        def add_part(e):
            src = c_from(e)
            remote(
                part_send.at[h, e], part_recv.at[h, src], part_send_sem.at[h, e],
                part_recv_sem.at[h, src], rep=c_at(e),
            ).wait_recv()
            own_part[h] += part_recv[h, src].astype(F32)

        each(1, C, add_part)
        agg_half = own_part[h].astype(BF16)
        agg_halves.append(agg_half)
        term = dot(agg_half, weight[cols(h)])
        pre = term if pre is None else pre + term

    sig = jax.nn.sigmoid(pre)
    grad_pre = (cot_ref[...].astype(F32) * sig * (1.0 + pre * (1.0 - sig))).astype(BF16)

    def grad_copy(h, e):
        return remote(
            grads.at[h, c], grads.at[h, c], grad_send_sem.at[h, e], grad_recv_sem.at[h, c],
            rep=c_at(e),
        )

    def make_grads(h):
        grads[h, c] = lax.dot_general(
            grad_pre, weight[cols(h)], (((1,), (1,)), ((), ())), preferred_element_type=F32
        ).astype(BF16)

    def send_grads(h):
        each(1, C, lambda e: grad_copy(h, e).start())

    def grad_wait(h):
        def one(e):
            src = c_from(e)
            remote(
                grads.at[h, src], grads.at[h, src], grad_send_sem.at[h, e],
                grad_recv_sem.at[h, src], rep=c_at(e),
            ).wait_recv()

        each(1, C, one)

    make_grads(0)
    send_grads(0)

    agg = jnp.concatenate(agg_halves, axis=1)
    w_part[...] = lax.dot_general(
        agg, grad_pre, (((0,), (0,)), ((), ())), preferred_element_type=F32
    ).reshape(w_part.shape)
    w_pair_send[...] = w_part[1 - k].astype(BF16)
    w_pair = to_partner(w_pair_send, w_pair_recv, w_pair_sem.at[0], w_pair_sem.at[1])
    w_pair.start()
    for h in range(1, halves):
        make_grads(h)
    act_ref[...] = (pre * sig).astype(BF16)
    w_pair.wait_recv()
    w_half[...] = w_part[k] + w_pair_recv[...].astype(F32)
    w_rep_send[...] = w_half[...].astype(BF16)

    def w_rep_copy(e):
        dst = c_at(e)
        return remote(
            w_rep_send.at[dst], w_rep_recv.at[c], w_rep_send_sem.at[e], w_rep_recv_sem.at[c],
            rep=dst,
        )

    each(1, C, lambda e: w_rep_copy(e).start())
    for h in range(1, halves):
        send_grads(h)

    def returned(h, q):
        return dot(bwd_adj[q], grads[h].reshape(C * B, W))

    def pair_copy(h, j):
        zz = z_at(j)
        return to_partner(
            pair_send.at[h, zz], pair_recv.at[h, zz], pair_send_sem.at[h, zz],
            pair_recv_sem.at[h, zz],
        )

    def ret_copy(h, d):
        return remote(
            ret_send.at[h, d], ret_recv.at[h, z], ret_send_sem.at[h, d], ret_recv_sem.at[h, z],
            row=2 * z_at(d) + k,
        )

    def w_z_copy(d):
        return remote(
            w_z.at[z], w_z.at[z], w_z_send_sem.at[d], w_z_recv_sem.at[z], row=2 * z_at(d) + k
        )

    def return_half(h):
        def send_pair(j):
            zz = z_at(j)
            pair_send[h, zz] = returned(h, 2 * zz + 1 - k).astype(BF16)
            pair_copy(h, j).start()

        def joined(j):
            zz = z_at(j)
            value = returned(h, 2 * zz + k)
            pair_copy(h, j).wait_recv()
            return value + pair_recv[h, zz].astype(F32)

        def send_ret(d):
            ret_send[h, d] = joined(d).astype(BF16)
            ret_copy(h, d).start()

        grad_wait(h)
        each(1, Z + 1, send_pair)
        each(1, Z, send_ret)
        fgrad_ref[:, cols(h)] = joined(Z)

    def add_w_rep(e):
        src = c_from(e)
        remote(
            w_rep_send.at[src], w_rep_recv.at[src], w_rep_send_sem.at[e], w_rep_recv_sem.at[src],
            rep=src,
        ).wait_recv()
        w_half[c] += w_rep_recv[src].astype(F32)

    return_half(0)
    each(1, C, add_w_rep)
    w_z[z] = w_half[c].astype(BF16)
    each(1, Z, lambda d: w_z_copy(d).start())
    for h in range(1, halves):
        return_half(h)

    def w_z_wait(d):
        src = z_from(d)
        remote(
            w_z.at[src], w_z.at[src], w_z_send_sem.at[d], w_z_recv_sem.at[src],
            row=2 * src + k,
        ).wait_recv()

    each(1, Z, w_z_wait)
    w_all[k, c] = jnp.sum(w_z[...].astype(F32), axis=0).astype(BF16)

    def w_gather_copy(e):
        return remote(
            w_all.at[k, c], w_all.at[k, c], w_gather_send_sem.at[e], w_gather_recv_sem.at[c],
            rep=c_at(e),
        )

    each(1, C, lambda e: w_gather_copy(e).start())

    def add_ret(h, d):
        src = z_from(d)
        remote(
            ret_send.at[h, d], ret_recv.at[h, src], ret_send_sem.at[h, d],
            ret_recv_sem.at[h, src], row=2 * src + k,
        ).wait_recv()
        fgrad_ref[:, cols(h)] += ret_recv[h, src].astype(F32)

    for h in range(halves - 1):
        each(1, Z, lambda d: add_ret(h, d))

    def w_gather_wait(e):
        src = c_from(e)
        remote(
            w_all.at[k, src], w_all.at[k, src], w_gather_send_sem.at[e],
            w_gather_recv_sem.at[src], rep=src,
        ).wait_recv()

    each(1, C, w_gather_wait)
    w_last = to_partner(w_all.at[k], w_all.at[k], w_last_sem.at[0], w_last_sem.at[1])
    w_last.start()
    each(1, Z, lambda d: add_ret(halves - 1, d))
    to_partner(w_all.at[1 - k], w_all.at[1 - k], w_last_sem.at[0], w_last_sem.at[1]).wait_recv()
    wgrad_ref[...] = w_all[...].astype(F32).reshape(wgrad_ref.shape)

    w_pair.wait_send()
    w_last.wait_send()
    each(1, Z, lambda d: w_z_copy(d).wait_send())
    for h in range(halves):
        feat_pairs[h].wait_send()
        pair_copy(h, Z).wait_send()

        def drain_z(d):
            feat_send(h, d).wait_send()
            feat_forward(h, d).wait_send()
            pair_copy(h, d).wait_send()
            ret_copy(h, d).wait_send()

        def drain_c(e):
            part_copy(h, e).wait_send()
            grad_copy(h, e).wait_send()

        each(1, Z, drain_z)
        each(1, C, drain_c)

    def drain_w(e):
        w_rep_copy(e).wait_send()
        w_gather_copy(e).wait_send()

    each(1, C, drain_w)


def write_out(*refs):
    count = len(refs) // 2
    sem = refs[-1]
    copies = [
        pltpu.make_async_copy(refs[i], refs[count + i], sem.at[i]) for i in range(count)
    ]
    for copy in copies:
        copy.start()
    for copy in copies:
        copy.wait()


def solution(mesh):
    R = mesh.shape["row"]
    C = mesh.shape["rep"]
    Z = R // 2

    def body(features, weight, cotangent, adjacency, tile_out, tile_in, live_count):
        B, F = features.shape
        S = adjacency.shape[2]
        H = F // (2 * C)
        N = 2
        W = F // N
        anywhere = pl.BlockSpec(memory_space=pl.ANY)
        vector = pl.BlockSpec(memory_space=pltpu.VMEM)
        dma = pltpu.SemaphoreType.DMA
        out_shape = (
            jax.ShapeDtypeStruct((B, F), BF16),
            jax.ShapeDtypeStruct(weight.shape, F32),
            jax.ShapeDtypeStruct((B, F), F32),
        )
        buffers = [
            ((S, B, B), BF16), ((S + 1, B, B), F32),
            ((Z, C * B, 2 * B), BF16), ((R, B, C * B), BF16),
            ((N, R, B, W), BF16), (weight.shape, BF16), ((B, F), BF16),
            ((C * B, W), F32), ((N, B, W), F32),
            ((N, C, B, W), BF16), ((N, C, B, W), BF16), ((N, C, B, W), BF16),
            ((N, Z, B, W), BF16), ((N, Z, B, W), BF16),
            ((N, Z, B, W), BF16), ((N, Z, B, W), BF16),
            ((2, C, H, F), F32), ((C, H, F), BF16), ((C, H, F), BF16), ((C, H, F), F32),
            ((C, H, F), BF16), ((C, H, F), BF16), ((Z, H, F), BF16), ((2, C, H, F), BF16),
        ]
        held = sum(math.prod(shape) * (4 if kind == F32 else 2) for shape, kind in buffers)
        results = pl.pallas_call(
            functools.partial(kernel, Z, C, S),
            out_shape=out_shape,
            in_specs=[pl.BlockSpec(memory_space=pltpu.HBM)] * 6
            + [pl.BlockSpec(memory_space=pltpu.SMEM)],
            out_specs=(vector, vector, vector),
            scratch_shapes=[pltpu.VMEM(shape, kind) for shape, kind in buffers] + [
                pltpu.SMEM(tile_out.shape, jnp.int32),
                pltpu.SMEM(tile_in.shape, jnp.int32),
                pltpu.SMEM((S,), jnp.int32),
                dma((6 + N,)), dma((N, Z)), dma((N, Z)), dma((N, R)),
                dma((N, C)), dma((N, C)), dma((N, C)), dma((N, C)),
                dma((N, Z)), dma((N, Z)), dma((N, Z)), dma((N, Z)),
                dma((2,)), dma((C,)), dma((C,)), dma((Z,)), dma((Z,)),
                dma((C,)), dma((C,)), dma((2,)),
            ],
            compiler_params=pltpu.CompilerParams(
                collective_id=0, has_side_effects=True,
                vmem_limit_bytes=min(held + 8 * 2 ** 20, 60 * 2 ** 20),
            ),
        )(*(
            pltpu.with_memory_space_constraint(arg, pltpu.HBM)
            for arg in (features, weight, cotangent, adjacency, tile_out, tile_in)
        ), live_count)
        return pl.pallas_call(
            write_out,
            out_shape=out_shape,
            in_specs=[vector] * 3,
            out_specs=(anywhere,) * 3,
            scratch_shapes=[dma((3,))],
            compiler_params=pltpu.CompilerParams(vmem_limit_bytes=4 * 2 ** 20),
        )(*results)

    return jax.shard_map(
        body,
        mesh=mesh,
        in_specs=(
            P(("row", "rep"), None),
            P(),
            P(("row", "rep"), None),
            P("row", "rep", None, None, None),
            P("row", "rep", None),
            P("row", "rep", None),
            P("row", "rep"),
        ),
        out_specs=(P(("row", "rep"), None), P(), P(("row", "rep"), None)),
        check_vma=False,
    )
```

```python
import functools
import math

import jax
import jax.numpy as jnp
from jax import lax
from jax.experimental import pallas as pl
from jax.experimental.pallas import tpu as pltpu
from jax.sharding import PartitionSpec as P

MESH = pl.DeviceIdType.MESH
F32 = jnp.float32
BF16 = jnp.bfloat16


def each(first, last, step):
    if last - first <= 4:
        for index in range(first, last):
            step(index)
    else:
        lax.fori_loop(first, last, lambda index, unused: (step(index), unused)[1], 0)


def dot(left, right):
    return jnp.dot(left, right, preferred_element_type=F32)


def kernel(
    Z, C, S,
    feat_hbm, weight_hbm, cot_hbm, adj_hbm, tout_hbm, tin_hbm, live_ref,
    act_ref, wgrad_ref, fgrad_ref,
    tiles, cum, fwd_adj, bwd_adj, feat, weight_ref, cot_ref,
    acc, own_part, part_send, part_recv, grads,
    pair_send, pair_recv, ret_send, ret_recv,
    w_part, w_pair_send, w_pair_recv, w_half, w_rep_send, w_rep_recv, w_z, w_all,
    tout_ref, tin_ref, pos,
    local_sem, feat_send_sem, feat_fwd_sem, feat_recv_sem,
    part_send_sem, part_recv_sem, grad_send_sem, grad_recv_sem,
    pair_send_sem, pair_recv_sem, ret_send_sem, ret_recv_sem,
    w_pair_sem, w_rep_send_sem, w_rep_recv_sem, w_z_send_sem, w_z_recv_sem,
    w_gather_send_sem, w_gather_recv_sem,
):
    r = lax.axis_index("row")
    c = lax.axis_index("rep")
    z = r // 2
    k = r % 2
    pr = 2 * z + 1 - k
    B = tiles.shape[1]
    W = feat.shape[3]
    halves = feat.shape[0]

    def cols(h):
        return slice(h * W, (h + 1) * W)

    def z_at(d):
        return (z + d) % Z

    def z_from(d):
        return (z + Z - d) % Z

    def c_at(e):
        return (c + e) % C

    def c_from(e):
        return (c + C - e) % C

    def remote(src, dst, send_sem, recv_sem, **where):
        return pltpu.make_async_remote_copy(
            src_ref=src, dst_ref=dst, send_sem=send_sem, recv_sem=recv_sem,
            device_id=where, device_id_type=MESH,
        )

    def to_partner(src, dst, send_sem, recv_sem):
        return remote(src, dst, send_sem, recv_sem, row=pr)

    barrier = pltpu.get_barrier_semaphore()

    def greet(**where):
        pl.semaphore_signal(barrier, inc=1, device_id=where, device_id_type=MESH)

    each(1, Z, lambda d: greet(row=2 * z_at(d) + k))
    each(1, C, lambda e: greet(rep=c_at(e)))
    greet(row=pr)
    each(1, C, lambda e: greet(row=pr, rep=c_at(e)))

    own_copies = [
        pltpu.make_async_copy(feat_hbm.at[:, cols(h)], feat.at[h, r], local_sem.at[6 + h])
        for h in range(halves)
    ]
    tile_copy = pltpu.make_async_copy(adj_hbm.at[0, 0], tiles, local_sem.at[0])
    weight_copy = pltpu.make_async_copy(weight_hbm, weight_ref, local_sem.at[1])
    cot_copy = pltpu.make_async_copy(cot_hbm, cot_ref, local_sem.at[2])
    id_copies = [
        pltpu.make_async_copy(tout_hbm, tout_ref, local_sem.at[3]),
        pltpu.make_async_copy(tin_hbm, tin_ref, local_sem.at[4]),
    ]
    for copy in id_copies + [tile_copy] + own_copies + [weight_copy, cot_copy]:
        copy.start()
    pl.semaphore_wait(barrier, 1 + (Z - 1) + 2 * (C - 1))

    def feat_send(h, d):
        return remote(
            feat_hbm.at[:, cols(h)], feat.at[h, r], feat_send_sem.at[h, d],
            feat_recv_sem.at[h, r], row=2 * z_at(d) + k,
        )

    def feat_forward(h, d):
        q = 2 * z_from(d) + k
        return to_partner(
            feat.at[h, q], feat.at[h, q], feat_fwd_sem.at[h, d], feat_recv_sem.at[h, q]
        )

    def feat_wait(h, q):
        to_partner(
            feat.at[h, q], feat.at[h, q], feat_fwd_sem.at[h, 0], feat_recv_sem.at[h, q]
        ).wait_recv()

    feat_pairs = [
        to_partner(
            feat_hbm.at[:, cols(h)], feat.at[h, r], feat_fwd_sem.at[h, 0], feat_recv_sem.at[h, r]
        )
        for h in range(halves)
    ]
    for h in range(halves):
        each(1, Z, lambda d: feat_send(h, d).start())
        feat_pairs[h].start()

    for copy in id_copies:
        copy.wait()
    live = live_ref[0, 0]
    for s in range(S):
        pos[s] = jnp.where(s < live, tin_ref[0, 0, s] * C + tout_ref[0, 0, s], -1)
    tile_copy.wait()
    cum[S] = jnp.zeros((B, B), F32)
    for s in range(S):
        prev = jnp.int32(S)
        for other in range(s):
            prev = jnp.where(pos[other] == pos[s], other, prev)
        term = tiles[s].astype(F32)
        cum[s] = term + cum[prev] if s else term

    def place(zz, unused):
        for kk in range(2):
            for b in range(C):
                spot = (2 * zz + kk) * C + b
                last = jnp.int32(S)
                for s in range(S):
                    last = jnp.where(pos[s] == spot, s, last)
                block = cum[last]
                fwd_adj[zz, b * B:(b + 1) * B, kk * B:(kk + 1) * B] = block.astype(BF16)
                bwd_adj[2 * zz + kk, :, b * B:(b + 1) * B] = block.T.astype(BF16)
        return unused

    lax.fori_loop(0, Z, place, 0)

    def pair_feats(h, zz):
        return feat[h, pl.ds(2 * zz, 2)].reshape(2 * B, W)

    def part_copy(h, e):
        return remote(
            part_send.at[h, e], part_recv.at[h, c], part_send_sem.at[h, e],
            part_recv_sem.at[h, c], rep=c_at(e),
        )

    end = z_from(Z - 1)
    for h in range(halves):
        own_copies[h].wait()
        feat_wait(h, pr)
        acc[...] = dot(fwd_adj[z], pair_feats(h, z))

        def take(d):
            feat_wait(h, 2 * z_from(d) + k)
            feat_forward(h, d).start()

        def add_chip(d):
            take(d + 1)
            zz = z_from(d)
            feat_wait(h, 2 * zz + 1 - k)
            acc[...] += dot(fwd_adj[zz], pair_feats(h, zz))

        take(1)
        each(1, Z - 1, add_chip)
        feat_wait(h, 2 * end + 1 - k)

        def part_of(b):
            rows = pl.ds(pl.multiple_of(b * B, B), B)
            return acc[rows] + dot(fwd_adj[end, rows], pair_feats(h, end))

        def send_part(e):
            part_send[h, e] = part_of(c_at(e)).astype(BF16)
            part_copy(h, e).start()

        each(1, C, send_part)
        own_part[h] = part_of(c)

    weight_copy.wait()
    cot_copy.wait()
    weight = weight_ref[...]
    pre = None
    agg_halves = []
    for h in range(halves):

        def add_part(e):
            src = c_from(e)
            remote(
                part_send.at[h, e], part_recv.at[h, src], part_send_sem.at[h, e],
                part_recv_sem.at[h, src], rep=c_at(e),
            ).wait_recv()
            own_part[h] += part_recv[h, src].astype(F32)

        each(1, C, add_part)
        agg_half = own_part[h].astype(BF16)
        agg_halves.append(agg_half)
        term = dot(agg_half, weight[cols(h)])
        pre = term if pre is None else pre + term

    sig = jax.nn.sigmoid(pre)
    grad_pre = (cot_ref[...].astype(F32) * sig * (1.0 + pre * (1.0 - sig))).astype(BF16)

    def grad_copy(h, e):
        return remote(
            grads.at[h, c], grads.at[h, c], grad_send_sem.at[h, e], grad_recv_sem.at[h, c],
            rep=c_at(e),
        )

    def make_grads(h):
        grads[h, c] = lax.dot_general(
            grad_pre, weight[cols(h)], (((1,), (1,)), ((), ())), preferred_element_type=F32
        ).astype(BF16)

    def send_grads(h):
        each(1, C, lambda e: grad_copy(h, e).start())

    def grad_wait(h):
        def one(e):
            src = c_from(e)
            remote(
                grads.at[h, src], grads.at[h, src], grad_send_sem.at[h, e],
                grad_recv_sem.at[h, src], rep=c_at(e),
            ).wait_recv()

        each(1, C, one)

    make_grads(0)
    send_grads(0)

    agg = jnp.concatenate(agg_halves, axis=1)
    w_part[...] = lax.dot_general(
        agg, grad_pre, (((0,), (0,)), ((), ())), preferred_element_type=F32
    ).reshape(w_part.shape)
    w_pair_send[...] = w_part[1 - k].astype(BF16)
    w_pair = to_partner(w_pair_send, w_pair_recv, w_pair_sem.at[0], w_pair_sem.at[1])
    w_pair.start()
    for h in range(1, halves):
        make_grads(h)
    act_ref[...] = (pre * sig).astype(BF16)
    w_pair.wait_recv()
    w_half[...] = w_part[k] + w_pair_recv[...].astype(F32)
    w_rep_send[...] = w_half[...].astype(BF16)

    def w_rep_copy(e):
        dst = c_at(e)
        return remote(
            w_rep_send.at[dst], w_rep_recv.at[c], w_rep_send_sem.at[e], w_rep_recv_sem.at[c],
            rep=dst,
        )

    each(1, C, lambda e: w_rep_copy(e).start())
    for h in range(1, halves):
        send_grads(h)

    def returned(h, q):
        return dot(bwd_adj[q], grads[h].reshape(C * B, W))

    def pair_copy(h, j):
        zz = z_at(j)
        return to_partner(
            pair_send.at[h, zz], pair_recv.at[h, zz], pair_send_sem.at[h, zz],
            pair_recv_sem.at[h, zz],
        )

    def ret_copy(h, d):
        return remote(
            ret_send.at[h, d], ret_recv.at[h, z], ret_send_sem.at[h, d], ret_recv_sem.at[h, z],
            row=2 * z_at(d) + k,
        )

    def w_z_copy(d):
        return remote(
            w_z.at[z], w_z.at[z], w_z_send_sem.at[d], w_z_recv_sem.at[z], row=2 * z_at(d) + k
        )

    def return_half(h):
        def send_pair(j):
            zz = z_at(j)
            pair_send[h, zz] = returned(h, 2 * zz + 1 - k).astype(BF16)
            pair_copy(h, j).start()

        def joined(j):
            zz = z_at(j)
            value = returned(h, 2 * zz + k)
            pair_copy(h, j).wait_recv()
            return value + pair_recv[h, zz].astype(F32)

        def send_ret(d):
            ret_send[h, d] = joined(d).astype(BF16)
            ret_copy(h, d).start()

        grad_wait(h)
        each(1, Z + 1, send_pair)
        each(1, Z, send_ret)
        fgrad_ref[:, cols(h)] = joined(Z)

    def add_w_rep(e):
        src = c_from(e)
        remote(
            w_rep_send.at[src], w_rep_recv.at[src], w_rep_send_sem.at[e], w_rep_recv_sem.at[src],
            rep=src,
        ).wait_recv()
        w_half[c] += w_rep_recv[src].astype(F32)

    each(1, C, add_w_rep)
    w_z[z] = w_half[c].astype(BF16)
    each(1, Z, lambda d: w_z_copy(d).start())
    return_half(0)
    for h in range(1, halves):
        return_half(h)

    def w_z_wait(d):
        src = z_from(d)
        remote(
            w_z.at[src], w_z.at[src], w_z_send_sem.at[d], w_z_recv_sem.at[src],
            row=2 * src + k,
        ).wait_recv()

    each(1, Z, w_z_wait)
    w_all[k, c] = jnp.sum(w_z[...].astype(F32), axis=0).astype(BF16)

    def w_gather_copy(kk, e):
        return remote(
            w_all.at[k, c], w_all.at[k, c], w_gather_send_sem.at[kk, e],
            w_gather_recv_sem.at[k, c], row=2 * z + (k + kk) % 2, rep=c_at(e),
        )

    def w_gather_wait(kk, e):
        src_k, src_c = (k + kk) % 2, c_from(e)
        remote(
            w_all.at[src_k, src_c], w_all.at[src_k, src_c], w_gather_send_sem.at[kk, e],
            w_gather_recv_sem.at[src_k, src_c], row=2 * z + src_k, rep=src_c,
        ).wait_recv()

    for kk in range(2):
        each(1 - kk, C, lambda e: w_gather_copy(kk, e).start())

    def add_ret(h, d):
        src = z_from(d)
        remote(
            ret_send.at[h, d], ret_recv.at[h, src], ret_send_sem.at[h, d],
            ret_recv_sem.at[h, src], row=2 * src + k,
        ).wait_recv()
        fgrad_ref[:, cols(h)] += ret_recv[h, src].astype(F32)

    for h in range(halves):
        each(1, Z, lambda d: add_ret(h, d))
    for kk in range(2):
        each(1 - kk, C, lambda e: w_gather_wait(kk, e))
    wgrad_ref[...] = w_all[...].astype(F32).reshape(wgrad_ref.shape)

    w_pair.wait_send()
    each(1, Z, lambda d: w_z_copy(d).wait_send())
    for h in range(halves):
        feat_pairs[h].wait_send()
        pair_copy(h, Z).wait_send()

        def drain_z(d):
            feat_send(h, d).wait_send()
            feat_forward(h, d).wait_send()
            pair_copy(h, d).wait_send()
            ret_copy(h, d).wait_send()

        def drain_c(e):
            part_copy(h, e).wait_send()
            grad_copy(h, e).wait_send()

        each(1, Z, drain_z)
        each(1, C, drain_c)

    each(1, C, lambda e: w_rep_copy(e).wait_send())
    for kk in range(2):
        each(1 - kk, C, lambda e: w_gather_copy(kk, e).wait_send())


def write_out(*refs):
    count = len(refs) // 2
    sem = refs[-1]
    copies = [
        pltpu.make_async_copy(refs[i], refs[count + i], sem.at[i]) for i in range(count)
    ]
    for copy in copies:
        copy.start()
    for copy in copies:
        copy.wait()


def solution(mesh):
    R = mesh.shape["row"]
    C = mesh.shape["rep"]
    Z = R // 2

    def body(features, weight, cotangent, adjacency, tile_out, tile_in, live_count):
        B, F = features.shape
        S = adjacency.shape[2]
        H = F // (2 * C)
        N = 2
        W = F // N
        anywhere = pl.BlockSpec(memory_space=pl.ANY)
        vector = pl.BlockSpec(memory_space=pltpu.VMEM)
        dma = pltpu.SemaphoreType.DMA
        out_shape = (
            jax.ShapeDtypeStruct((B, F), BF16),
            jax.ShapeDtypeStruct(weight.shape, F32),
            jax.ShapeDtypeStruct((B, F), F32),
        )
        buffers = [
            ((S, B, B), BF16), ((S + 1, B, B), F32),
            ((Z, C * B, 2 * B), BF16), ((R, B, C * B), BF16),
            ((N, R, B, W), BF16), (weight.shape, BF16), ((B, F), BF16),
            ((C * B, W), F32), ((N, B, W), F32),
            ((N, C, B, W), BF16), ((N, C, B, W), BF16), ((N, C, B, W), BF16),
            ((N, Z, B, W), BF16), ((N, Z, B, W), BF16),
            ((N, Z, B, W), BF16), ((N, Z, B, W), BF16),
            ((2, C, H, F), F32), ((C, H, F), BF16), ((C, H, F), BF16), ((C, H, F), F32),
            ((C, H, F), BF16), ((C, H, F), BF16), ((Z, H, F), BF16), ((2, C, H, F), BF16),
        ]
        held = sum(math.prod(shape) * (4 if kind == F32 else 2) for shape, kind in buffers)
        results = pl.pallas_call(
            functools.partial(kernel, Z, C, S),
            out_shape=out_shape,
            in_specs=[pl.BlockSpec(memory_space=pltpu.HBM)] * 6
            + [pl.BlockSpec(memory_space=pltpu.SMEM)],
            out_specs=(vector, vector, vector),
            scratch_shapes=[pltpu.VMEM(shape, kind) for shape, kind in buffers] + [
                pltpu.SMEM(tile_out.shape, jnp.int32),
                pltpu.SMEM(tile_in.shape, jnp.int32),
                pltpu.SMEM((S,), jnp.int32),
                dma((6 + N,)), dma((N, Z)), dma((N, Z)), dma((N, R)),
                dma((N, C)), dma((N, C)), dma((N, C)), dma((N, C)),
                dma((N, Z)), dma((N, Z)), dma((N, Z)), dma((N, Z)),
                dma((2,)), dma((C,)), dma((C,)), dma((Z,)), dma((Z,)),
                dma((2, C)), dma((2, C)),
            ],
            compiler_params=pltpu.CompilerParams(
                collective_id=0, has_side_effects=True,
                vmem_limit_bytes=min(held + 8 * 2 ** 20, 60 * 2 ** 20),
            ),
        )(*(
            pltpu.with_memory_space_constraint(arg, pltpu.HBM)
            for arg in (features, weight, cotangent, adjacency, tile_out, tile_in)
        ), live_count)
        return pl.pallas_call(
            write_out,
            out_shape=out_shape,
            in_specs=[vector] * 3,
            out_specs=(anywhere,) * 3,
            scratch_shapes=[dma((3,))],
            compiler_params=pltpu.CompilerParams(vmem_limit_bytes=4 * 2 ** 20),
        )(*results)

    return jax.shard_map(
        body,
        mesh=mesh,
        in_specs=(
            P(("row", "rep"), None),
            P(),
            P(("row", "rep"), None),
            P("row", "rep", None, None, None),
            P("row", "rep", None),
            P("row", "rep", None),
            P("row", "rep"),
        ),
        out_specs=(P(("row", "rep"), None), P(), P(("row", "rep"), None)),
        check_vma=False,
    )
```
